32 devices in a mesh: row: 8 (over z, y), col: 4 (over x, core).
Axes of the slice: x: 2, y: 2, z: 4, core: 2. Of those that a mesh axis runs over, the one named last changes fastest.
Arguments:
- rhs_grid: float32 [65536, 512], P(('row', 'col')), may hold values from -6 to 6
- leaf_order: int32 [128, 512], P(('row', 'col')), may hold values from 0 to 511, each once within a row
- source_basis: float32 [128, 512, 192], P(('row', 'col')), may hold values from -0.25 to 0.25
- transfer: float32 [7, 128, 192, 384], P(None, ('row', 'col')), may hold values from -0.3125 to 0.3125
- target_basis: float32 [128, 512, 192], P(('row', 'col')), may hold values from -0.4375 to 0.4375
Outputs:
- result: float32 [65536, 512], P(('row', 'col'))
The draws below stay inside these ranges and needn't reach their ends.
Inputs may be any that keep to these rules, and one draw needn't show every extreme that they name: Each row of leaf_order names every one of 0 to 511 once.
All inputs are finite; a program needn't handle non-finite values.
Results may differ from the reference program's by a relative error of at most 0.00013.
Values sent between devices are 32-bit elements; how exact they have to be, the bound alone decides.
A program may use at most 128 MiB of HBM per device.

```python
import jax
import jax.numpy as jnp
from jax import lax

LEAF = 512
RANK = 192
RHS = 512
LOCAL_BITS = 2
ROW_BITS = 3
COL_BITS = 2
LEVELS = 7
LEAVES = 128
NPTS = 65536


def block_scale(key, dims, pieces, least, largest):
    def one(axis_at, shards_of):
        heights = jax.random.uniform(jax.random.fold_in(jax.random.fold_in(key, 6), axis_at), (shards_of,), jnp.float32, least / len(pieces), largest / len(pieces))
        return jnp.repeat(jnp.exp(heights), dims[axis_at] // shards_of).reshape((-1,) + (1,) * (len(dims) - axis_at - 1))

    gain = one(*pieces[0])
    for cut in pieces[1:]:
        gain = gain * one(*cut)
    return gain


def gaussian(key, dims, deviation, reach, cuts=(), dtype=jnp.bfloat16):
    values = deviation * jax.random.normal(key, dims, jnp.float32)
    if cuts:
        values = values * block_scale(key, dims, cuts, -0.22, 0.18)
    return jnp.clip(values, -reach, reach).astype(dtype)


def setup_inputs(seed: int = 0) -> dict:
    key_of = jax.random.split(jax.random.key(seed), 6)
    return {
        "rhs_grid": gaussian(key_of[0], (NPTS, RHS), 1.0, 6.0, ((0, 32),), jnp.float32),
        "leaf_order": jax.vmap(lambda own: jax.random.permutation(own, LEAF))(jax.random.split(key_of[1], LEAVES)).reshape((LEAVES, LEAF)).astype(jnp.int32),
        "source_basis": gaussian(key_of[2], (LEAVES, LEAF, RANK), LEAF ** -0.5, 0.25, ((0, 32),), jnp.float32),
        "transfer": gaussian(key_of[3], (LEVELS, LEAVES, RANK, 2 * RANK), (2 * RANK) ** -0.5, 0.3125, ((1, 32),), jnp.float32),
        "target_basis": gaussian(key_of[4], (LEAVES, LEAF, RANK), RANK ** -0.5, 0.4375, ((0, 32),), jnp.float32),
    }


PRECISE = lax.Precision.HIGHEST


def partner_of(values, bit_pos):
    node_count = values.shape[0]
    halves = values.reshape((node_count // (2 ** (bit_pos + 1)), 2, 2 ** bit_pos) + values.shape[1:])
    return halves[:, ::-1].reshape(values.shape)


def place_rows(basis, order):
    def single(leaf_block, leaf_index):
        return jnp.zeros_like(leaf_block).at[leaf_index].set(leaf_block)
    return jax.vmap(single)(basis, order)


def reference(rhs_grid, leaf_order, source_basis, transfer, target_basis):
    bit_order = list(range(LOCAL_BITS)) + [LOCAL_BITS + COL_BITS + offset for offset in range(ROW_BITS)] + [LOCAL_BITS + offset for offset in range(COL_BITS)]
    placed_in = place_rows(source_basis, leaf_order)
    current = jnp.einsum("lqk,lqr->lkr", placed_in, rhs_grid.reshape(LEAVES, LEAF, RHS), precision=PRECISE)
    for section in range(LEVELS):
        blocks = transfer[section]
        other = partner_of(current, bit_order[section])
        own_term = jnp.einsum("nij,njr->nir", blocks[:, :, :RANK], current, precision=PRECISE)
        current = own_term + jnp.einsum("nij,njr->nir", blocks[:, :, RANK:], other, precision=PRECISE)
    placed_out = place_rows(target_basis, leaf_order)
    result = jnp.einsum("lqk,lkr->lqr", placed_out, current, precision=PRECISE)
    return result.reshape(NPTS, RHS)
```

```python
import functools

import jax
import jax.numpy as jnp
from jax import lax
from jax.experimental import pallas as pl
from jax.experimental.pallas import tpu as pltpu
from jax.sharding import PartitionSpec as P

F32 = jnp.float32
BF16 = jnp.bfloat16
WIDTH = 128
MIDDLE = 2
FAR = 3
LEAD = 2
SLOTS = 4
VMEM_BYTES = 67043328


def split(value):
    high = value.astype(BF16)
    return high, (value - high.astype(F32)).astype(BF16)


def dot(a, b):
    return jnp.dot(a, b, preferred_element_type=F32)


def dot3(a_high, a_low, b):
    b_high, b_low = split(b)
    width = b.shape[1]
    both = dot(a_high, jnp.concatenate([b_high, b_low], axis=1))
    return both[:, :width] + (both[:, width:] + dot(a_low, b_high))


def partner_id(axis, bit_pos):
    mask = 2**bit_pos
    here = lax.axis_index(axis)
    return {axis: here + mask * (1 - 2 * ((here // mask) % 2))}


def kernel(
    stages, offsets, low_bits,
    rhs, order, source, transfer, target, out,
    order_v, chosen, rhs_v, source_v, target_v, transfer_v, local_t, stage_t, in_v, placed_v,
    sent, received, order_sem, rhs_sem, load_sem, transfer_sem, send_sem, recv_sem,
):
    leaf_count, leaf_rows = order.shape
    chunks = rhs_v.shape[0]
    units = leaf_count * chunks
    levels = transfer.shape[0]
    rank = source_v.shape[1]
    count = len(stages)

    load_order = pltpu.make_async_copy(order, order_v, order_sem)
    load_target = pltpu.make_async_copy(target, target_v, load_sem.at[leaf_count])

    def load_source(leaf):
        return pltpu.make_async_copy(source.at[leaf], source_v.at[leaf], load_sem.at[leaf])

    def load_rhs(chunk):
        return pltpu.make_async_copy(
            rhs.at[:, pl.ds(pl.multiple_of(chunk * WIDTH, WIDTH), WIDTH)], rhs_v.at[chunk], rhs_sem.at[chunk]
        )

    def load_transfer(level):
        return pltpu.make_async_copy(transfer.at[level], transfer_v.at[level % SLOTS], transfer_sem.at[level])

    def select(leaf):
        grid_row = lax.broadcasted_iota(jnp.int32, (leaf_rows, leaf_rows), 0)
        named = jnp.broadcast_to(order_v[pl.ds(leaf, 1), :], (leaf_rows, leaf_rows))
        chosen[leaf] = jnp.where(grid_row == named, 1.0, 0.0).astype(BF16)

    def place_in(leaf):
        parts = jnp.concatenate(split(source_v[leaf]), axis=0)
        in_v[leaf] = lax.dot_general(
            parts, chosen[leaf], (((1,), (1,)), ((), ())), preferred_element_type=F32
        ).astype(BF16)

    def place_out(leaf):
        for index, part in enumerate(split(target_v[leaf])):
            placed_v[leaf, index] = lax.dot_general(
                chosen[leaf], part, (((1,), (1,)), ((), ())), preferred_element_type=F32
            ).astype(BF16)

    def prepare_local(level):
        load_transfer(level).wait()
        for node in range(leaf_count):
            for index, part in enumerate(split(transfer_v[level % SLOTS, node])):
                local_t[level, node, index] = part

    def prepare(stage):
        level = low_bits + stage
        load_transfer(level).wait()

        @pl.loop(0, leaf_count)
        def _(node):
            for index, part in enumerate(split(transfer_v[level % SLOTS, node])):
                stage_t[stage, node, index, 0] = part[:, :rank]
                stage_t[stage, node, index, 1] = part[:, rank:]

        if level + SLOTS < levels:
            load_transfer(level + SLOTS).start()

    def exchange(stage, unit):
        return pltpu.make_async_remote_copy(
            src_ref=sent.at[stage, unit],
            dst_ref=received.at[stage, unit],
            send_sem=send_sem.at[stage, unit],
            recv_sem=recv_sem.at[stage, unit],
            device_id=partner_id(*stages[stage]),
            device_id_type=pl.DeviceIdType.MESH,
        )

    def half(stage, node, side, value):
        return dot3(stage_t[stage, node, 0, side], stage_t[stage, node, 1, side], value)

    def combine(level, node, own, other):
        return dot3(local_t[level, node, 0], local_t[level, node, 1], jnp.concatenate([own, other], axis=0))

    def enter(chunk, first=False):
        load_rhs(chunk).wait()
        current = {}
        for leaf in range(leaf_count):
            rows = rhs_v[chunk, pl.ds(leaf * leaf_rows, leaf_rows), :]
            current[0, leaf] = dot3(in_v[leaf, :rank], in_v[leaf, rank:], rows)

        def value_of(level, node):
            if (level, node) not in current:
                bit = level - 1
                if first and all((level, other) not in current for other in range(leaf_count)):
                    prepare_local(bit)
                current[level, node] = combine(bit, node, value_of(bit, node), value_of(bit, node ^ 2**bit))
            return current[level, node]

        for node in range(leaf_count):
            unit = chunk * leaf_count + node
            sent[0, unit] = value_of(low_bits, node)
            if first and node == 0:
                pl.semaphore_wait(barrier, count)
            if first and node < LEAD:
                exchange(0, unit).start()

    def advance(stage, unit):
        node = unit % leaf_count
        own = half(stage, node, 0, sent[stage, unit])
        exchange(stage, unit).wait_recv()
        value = own + half(stage, node, 1, received[stage, unit])
        if stage + 1 < count:
            sent[stage + 1, unit] = value
            exchange(stage + 1, unit).start()
        else:
            chunk = unit // leaf_count
            rows = pl.ds(pl.multiple_of(node * leaf_rows, leaf_rows), leaf_rows)
            cols = pl.ds(pl.multiple_of(chunk * WIDTH, WIDTH), WIDTH)
            out[rows, cols] = dot3(placed_v[node, 0], placed_v[node, 1], value)

    load_order.start()
    for leaf in range(leaf_count):
        load_source(leaf).start()
    load_rhs(0).start()
    barrier = pltpu.get_barrier_semaphore()
    for stage in stages:
        pl.semaphore_signal(barrier, inc=1, device_id=partner_id(*stage), device_id_type=pl.DeviceIdType.MESH)
    load_order.wait()
    for level in range(low_bits):
        load_transfer(level).start()
    for leaf in range(leaf_count):
        select(leaf)
    for leaf in range(leaf_count):
        load_source(leaf).wait()
        place_in(leaf)
    for level in range(low_bits, min(SLOTS, levels)):
        load_transfer(level).start()
    load_rhs(1).start()
    enter(0, first=True)
    for level in range(SLOTS, min(SLOTS + low_bits, levels)):
        load_transfer(level).start()
    load_target.start()
    for chunk in range(2, chunks):
        load_rhs(chunk).start()
    prepare(0)
    prepare(1)
    enter(1)

    near = [stage for stage in range(count) if stages[stage] == ("col", 0)]
    turns = near + [stage for stage in reversed(range(count)) if stage not in near]

    @pl.loop(0, units + offsets[-1])
    def _(tick):
        @pl.when(tick + LEAD < units)
        def _():
            exchange(0, tick + LEAD).start()

        for stage in turns:
            unit = tick - offsets[stage]

            @pl.when((unit >= 0) & (unit < units))
            def _():
                advance(stage, unit)

        for stage in range(2, count):

            @pl.when(tick == stage - 2)
            def _():
                prepare(stage)

        @pl.when((tick >= offsets[-1] - leaf_count) & (tick < offsets[-1]))
        def _():
            leaf = tick - (offsets[-1] - leaf_count)

            @pl.when(leaf == 0)
            def _():
                load_target.wait()

            place_out(leaf)

        @pl.when((tick % leaf_count == 1) & (tick // leaf_count + 2 < chunks))
        def _():
            enter(tick // leaf_count + 2)

        done = tick - offsets[-1] - 1

        @pl.when(done >= 0)
        def _():
            for stage in range(count):
                exchange(stage, done).wait_send()

    for stage in range(count):
        exchange(stage, units - 1).wait_send()


def output_kernel(result, out, sem):
    pieces = sem.shape[0]
    rows = out.shape[0] // pieces

    def store(piece):
        at = pl.ds(piece * rows, rows)
        return pltpu.make_async_copy(result.at[at, :], out.at[at, :], sem.at[piece])

    for piece in range(pieces):
        store(piece).start()
    for piece in range(pieces):
        store(piece).wait()


def on_device(rhs_grid, leaf_order, source_basis, transfer, target_basis):
    leaf_count, leaf_rows = leaf_order.shape
    points, columns = rhs_grid.shape
    rank = source_basis.shape[2]
    levels = transfer.shape[0]
    low_bits = leaf_count.bit_length() - 1
    row_bits = lax.axis_size("row").bit_length() - 1
    col_bits = lax.axis_size("col").bit_length() - 1
    stages = [("row", bit) for bit in range(row_bits)] + [("col", bit) for bit in range(col_bits)]
    count = len(stages)
    offsets = [0]
    for axis, bit in stages[1:]:
        if axis == "col":
            offsets.append(offsets[-1] + 1)
        else:
            offsets.append(offsets[-1] + (FAR if bit == row_bits - 1 else MIDDLE))
    chunks = columns // WIDTH
    units = leaf_count * chunks
    hbm = pl.BlockSpec(memory_space=pl.ANY)
    vmem = pl.BlockSpec(memory_space=pltpu.VMEM)
    result = pl.pallas_call(
        functools.partial(kernel, stages, offsets, low_bits),
        out_shape=pltpu.VMEM((points, columns), F32),
        in_specs=[hbm, hbm, hbm, hbm, hbm],
        out_specs=vmem,
        scratch_shapes=[
            pltpu.VMEM((leaf_count, leaf_rows), jnp.int32),
            pltpu.VMEM((leaf_count, leaf_rows, leaf_rows), BF16),
            pltpu.VMEM((chunks, points, WIDTH), F32),
            pltpu.VMEM((leaf_count, rank, leaf_rows), F32),
            pltpu.VMEM((leaf_count, rank, leaf_rows), F32),
            pltpu.VMEM((SLOTS,) + transfer.shape[1:], F32),
            pltpu.VMEM((low_bits, leaf_count, 2, rank, 2 * rank), BF16),
            pltpu.VMEM((count, leaf_count, 2, 2, rank, rank), BF16),
            pltpu.VMEM((leaf_count, 2 * rank, leaf_rows), BF16),
            pltpu.VMEM((leaf_count, 2, leaf_rows, rank), BF16),
            pltpu.VMEM((count, units, rank, WIDTH), F32),
            pltpu.VMEM((count, units, rank, WIDTH), F32),
            pltpu.SemaphoreType.DMA,
            pltpu.SemaphoreType.DMA((chunks,)),
            pltpu.SemaphoreType.DMA((leaf_count + 1,)),
            pltpu.SemaphoreType.DMA((levels,)),
            pltpu.SemaphoreType.DMA((count, units)),
            pltpu.SemaphoreType.DMA((count, units)),
        ],
        compiler_params=pltpu.CompilerParams(
            collective_id=0, has_side_effects=True, vmem_limit_bytes=VMEM_BYTES - 4 * points * columns - 2**18
        ),
    )(rhs_grid, leaf_order, source_basis.swapaxes(1, 2), transfer, target_basis.swapaxes(1, 2))
    return pl.pallas_call(
        output_kernel,
        out_shape=jax.ShapeDtypeStruct((points, columns), F32),
        in_specs=[vmem],
        out_specs=hbm,
        scratch_shapes=[pltpu.SemaphoreType.DMA((2 * leaf_count,))],
        compiler_params=pltpu.CompilerParams(vmem_limit_bytes=2**20),
    )(result)


def solution(mesh):
    in_specs = (
        P(("row", "col"), None),
        P(("row", "col"), None),
        P(("row", "col"), None, None),
        P(None, ("row", "col"), None, None),
        P(("row", "col"), None, None),
    )
    out_specs = P(("row", "col"), None)
    return jax.shard_map(
        on_device, mesh=mesh, in_specs=in_specs, out_specs=out_specs, check_vma=False
    )
```

```python
import functools

import jax
import jax.numpy as jnp
from jax import lax
from jax.experimental import pallas as pl
from jax.experimental.pallas import tpu as pltpu
from jax.sharding import PartitionSpec as P

F32 = jnp.float32
BF16 = jnp.bfloat16
WIDTH = 128
MIDDLE = 2
FAR = 3
SLOTS = 4
LEAD = 1
FLIGHT = 8
VMEM_BYTES = 67043328


def split(value):
    high = value.astype(BF16)
    return high, (value - high.astype(F32)).astype(BF16)


def dot(a, b):
    return jnp.dot(a, b, preferred_element_type=F32)


def dot3(a_high, a_low, b):
    b_high, b_low = split(b)
    width = b.shape[1]
    both = dot(a_high, jnp.concatenate([b_high, b_low], axis=1))
    return both[:, :width] + (both[:, width:] + dot(a_low, b_high))


def partner_id(axis, bit_pos):
    mask = 2**bit_pos
    here = lax.axis_index(axis)
    return {axis: here + mask * (1 - 2 * ((here // mask) % 2))}


def kernel(
    stages, offsets, low_bits,
    rhs, order, source, transfer, target, out,
    order_v, chosen, rhs_v, source_v, target_v, transfer_v, local_t, stage_t, in_v, placed_v,
    sent, received, load_sem, rhs_sem, transfer_sem, send_sem, recv_sem,
):
    leaf_count, leaf_rows = order.shape
    chunks = rhs_v.shape[0]
    units = leaf_count * chunks
    levels = transfer.shape[0]
    rank = source_v.shape[1]
    count = len(stages)

    load_order = pltpu.make_async_copy(order, order_v, load_sem.at[0])
    load_source = pltpu.make_async_copy(source, source_v, load_sem.at[1])
    load_target = pltpu.make_async_copy(target, target_v, load_sem.at[2])

    def load_rhs(chunk):
        return pltpu.make_async_copy(
            rhs.at[:, pl.ds(pl.multiple_of(chunk * WIDTH, WIDTH), WIDTH)], rhs_v.at[chunk], rhs_sem.at[chunk]
        )

    def load_transfer(level):
        return pltpu.make_async_copy(
            transfer.at[level], transfer_v.at[level % SLOTS], transfer_sem.at[max(level - low_bits + 1, 0)]
        )

    low_slots = transfer_v.at[pl.ds(0, low_bits)]
    low_transfer = pltpu.make_async_copy(low_slots, low_slots, transfer_sem.at[0])

    def select(leaf):
        grid_row = lax.broadcasted_iota(jnp.int32, (leaf_rows, leaf_rows), 0)
        named = jnp.broadcast_to(order_v[pl.ds(leaf, 1), :], (leaf_rows, leaf_rows))
        chosen[leaf] = jnp.where(grid_row == named, 1.0, 0.0).astype(BF16)

    def place_in(leaf):
        parts = jnp.concatenate(split(source_v[leaf]), axis=0)
        in_v[leaf] = lax.dot_general(
            parts, chosen[leaf], (((1,), (1,)), ((), ())), preferred_element_type=F32
        ).astype(BF16)

    def place_out(leaf):
        for index, part in enumerate(split(target_v[leaf])):
            placed_v[leaf, index] = lax.dot_general(
                chosen[leaf], part, (((1,), (1,)), ((), ())), preferred_element_type=F32
            ).astype(BF16)

    def prepare_local(level):
        for node in range(leaf_count):
            for index, part in enumerate(split(transfer_v[level % SLOTS, node])):
                local_t[level, node, index] = part

    def prepare(stage):
        level = low_bits + stage
        load_transfer(level).wait()

        @pl.loop(0, leaf_count)
        def _(node):
            for index, part in enumerate(split(transfer_v[level % SLOTS, node])):
                stage_t[stage, node, index, 0] = part[:, :rank]
                stage_t[stage, node, index, 1] = part[:, rank:]

        if level + SLOTS < levels:
            load_transfer(level + SLOTS).start()

    def exchange(stage, unit):
        return pltpu.make_async_remote_copy(
            src_ref=sent.at[stage, unit],
            dst_ref=received.at[stage, unit],
            send_sem=send_sem,
            recv_sem=recv_sem.at[stage, unit % FLIGHT],
            device_id=partner_id(*stages[stage]),
            device_id_type=pl.DeviceIdType.MESH,
        )

    def half(stage, node, side, value):
        return dot3(stage_t[stage, node, 0, side], stage_t[stage, node, 1, side], value)

    def combine(level, node, own, other):
        return dot3(local_t[level, node, 0], local_t[level, node, 1], jnp.concatenate([own, other], axis=0))

    def enter(chunk, first=False):
        load_rhs(chunk).wait()
        current = {}
        for leaf in range(leaf_count):
            rows = rhs_v[chunk, pl.ds(leaf * leaf_rows, leaf_rows), :]
            current[0, leaf] = dot3(in_v[leaf, :rank], in_v[leaf, rank:], rows)

        def value_of(level, node):
            if (level, node) not in current:
                bit = level - 1
                if first and all((level, other) not in current for other in range(leaf_count)):
                    prepare_local(bit)
                current[level, node] = combine(bit, node, value_of(bit, node), value_of(bit, node ^ 2**bit))
            return current[level, node]

        for node in range(leaf_count):
            unit = chunk * leaf_count + node
            sent[0, unit] = value_of(low_bits, node)
            if first and node == 0:
                pl.semaphore_wait(barrier, count)
            if first and node < LEAD:
                exchange(0, unit).start()

    def advance(stage, unit):
        node = unit % leaf_count
        own = half(stage, node, 0, sent[stage, unit])
        exchange(stage, unit).wait_recv()
        if stage == 0:

            @pl.when(unit + LEAD < units)
            def _():
                exchange(0, unit + LEAD).start()

        value = own + half(stage, node, 1, received[stage, unit])
        if stage + 1 < count:
            sent[stage + 1, unit] = value
            exchange(stage + 1, unit).start()
        else:
            chunk = unit // leaf_count
            rows = pl.ds(pl.multiple_of(node * leaf_rows, leaf_rows), leaf_rows)
            cols = pl.ds(pl.multiple_of(chunk * WIDTH, WIDTH), WIDTH)
            out[rows, cols] = dot3(placed_v[node, 0], placed_v[node, 1], value)

    load_order.start()
    load_source.start()
    load_rhs(0).start()
    barrier = pltpu.get_barrier_semaphore()
    for stage in stages:
        pl.semaphore_signal(barrier, inc=1, device_id=partner_id(*stage), device_id_type=pl.DeviceIdType.MESH)
    load_order.wait()
    for level in range(low_bits):
        load_transfer(level).start()
    for leaf in range(leaf_count):
        select(leaf)
    load_source.wait()
    for leaf in range(leaf_count):
        place_in(leaf)
    for level in range(low_bits, min(SLOTS, levels)):
        load_transfer(level).start()
    load_rhs(1).start()
    if low_bits:
        low_transfer.wait()
    enter(0, first=True)
    for level in range(SLOTS, min(SLOTS + low_bits, levels)):
        load_transfer(level).start()
    load_target.start()
    for chunk in range(2, chunks):
        load_rhs(chunk).start()
    prepare(0)
    prepare(1)

    near = [stage for stage in range(count) if stages[stage] == ("col", 0)]
    turns = near + [stage for stage in reversed(range(count)) if stage not in near]

    @pl.loop(0, units + offsets[-1])
    def _(tick):
        for stage in turns:
            unit = tick - offsets[stage]

            @pl.when((unit >= 0) & (unit < units))
            def _():
                advance(stage, unit)

        for stage in range(2, count):

            @pl.when(tick == stage - 2)
            def _():
                prepare(stage)

        @pl.when((tick >= offsets[-1] - leaf_count) & (tick < offsets[-1]))
        def _():
            leaf = tick - (offsets[-1] - leaf_count)

            @pl.when(leaf == 0)
            def _():
                load_target.wait()

            place_out(leaf)

        @pl.when((tick % leaf_count == 1) & (tick // leaf_count + 1 < chunks))
        def _():
            enter(tick // leaf_count + 1)

    pltpu.make_async_copy(sent, sent, send_sem).wait()


def output_kernel(result, out, sem):
    pieces = sem.shape[0]
    rows = out.shape[0] // pieces

    def store(piece):
        at = pl.ds(piece * rows, rows)
        return pltpu.make_async_copy(result.at[at, :], out.at[at, :], sem.at[piece])

    for piece in range(pieces):
        store(piece).start()
    for piece in range(pieces):
        store(piece).wait()


def on_device(rhs_grid, leaf_order, source_basis, transfer, target_basis):
    leaf_count, leaf_rows = leaf_order.shape
    points, columns = rhs_grid.shape
    rank = source_basis.shape[2]
    levels = transfer.shape[0]
    low_bits = leaf_count.bit_length() - 1
    row_bits = lax.axis_size("row").bit_length() - 1
    col_bits = lax.axis_size("col").bit_length() - 1
    stages = [("row", bit) for bit in range(row_bits)] + [("col", bit) for bit in range(col_bits)]
    count = len(stages)
    offsets = [0]
    for axis, bit in stages[1:]:
        if axis == "col":
            offsets.append(offsets[-1] + 1)
        else:
            offsets.append(offsets[-1] + (FAR if bit == row_bits - 1 else MIDDLE))
    chunks = columns // WIDTH
    units = leaf_count * chunks
    hbm = pl.BlockSpec(memory_space=pl.ANY)
    vmem = pl.BlockSpec(memory_space=pltpu.VMEM)
    result = pl.pallas_call(
        functools.partial(kernel, stages, offsets, low_bits),
        out_shape=pltpu.VMEM((points, columns), F32),
        in_specs=[hbm, hbm, hbm, hbm, hbm],
        out_specs=vmem,
        scratch_shapes=[
            pltpu.VMEM((leaf_count, leaf_rows), jnp.int32),
            pltpu.VMEM((leaf_count, leaf_rows, leaf_rows), BF16),
            pltpu.VMEM((chunks, points, WIDTH), F32),
            pltpu.VMEM((leaf_count, rank, leaf_rows), F32),
            pltpu.VMEM((leaf_count, rank, leaf_rows), F32),
            pltpu.VMEM((SLOTS,) + transfer.shape[1:], F32),
            pltpu.VMEM((low_bits, leaf_count, 2, rank, 2 * rank), BF16),
            pltpu.VMEM((count, leaf_count, 2, 2, rank, rank), BF16),
            pltpu.VMEM((leaf_count, 2 * rank, leaf_rows), BF16),
            pltpu.VMEM((leaf_count, 2, leaf_rows, rank), BF16),
            pltpu.VMEM((count, units, rank, WIDTH), F32),
            pltpu.VMEM((count, units, rank, WIDTH), F32),
            pltpu.SemaphoreType.DMA((3,)),
            pltpu.SemaphoreType.DMA((chunks,)),
            pltpu.SemaphoreType.DMA((count + 1,)),
            pltpu.SemaphoreType.DMA,
            pltpu.SemaphoreType.DMA((count, FLIGHT)),
        ],
        compiler_params=pltpu.CompilerParams(
            collective_id=0, has_side_effects=True, vmem_limit_bytes=VMEM_BYTES - 4 * points * columns - 2**18
        ),
    )(rhs_grid, leaf_order, source_basis.swapaxes(1, 2), transfer, target_basis.swapaxes(1, 2))
    return pl.pallas_call(
        output_kernel,
        out_shape=jax.ShapeDtypeStruct((points, columns), F32),
        in_specs=[vmem],
        out_specs=hbm,
        scratch_shapes=[pltpu.SemaphoreType.DMA((2 * leaf_count,))],
        compiler_params=pltpu.CompilerParams(vmem_limit_bytes=2**20),
    )(result)


def solution(mesh):
    in_specs = (
        P(("row", "col"), None),
        P(("row", "col"), None),
        P(("row", "col"), None, None),
        P(None, ("row", "col"), None, None),
        P(("row", "col"), None, None),
    )
    out_specs = P(("row", "col"), None)
    return jax.shard_map(
        on_device, mesh=mesh, in_specs=in_specs, out_specs=out_specs, check_vma=False
    )
```

```python
import functools

import jax
import jax.numpy as jnp
from jax import lax
from jax.experimental import pallas as pl
from jax.experimental.pallas import tpu as pltpu
from jax.sharding import PartitionSpec as P

F32 = jnp.float32
BF16 = jnp.bfloat16
WIDTH = 128
MIDDLE = 2
FAR = 3
NEAR = 1
LAST = 1
LEAD = 1
FLIGHT = 8
VMEM_BYTES = 67043328


def split(value):
    high = value.astype(BF16)
    return high, (value - high.astype(F32)).astype(BF16)


def dot(a, b):
    return jnp.dot(a, b, preferred_element_type=F32)


def dot3(a_high, a_low, b):
    b_high, b_low = split(b)
    width = b.shape[1]
    both = dot(a_high, jnp.concatenate([b_high, b_low], axis=1))
    return both[:, :width] + (both[:, width:] + dot(a_low, b_high))


def partner_id(axis, bit_pos):
    mask = 2**bit_pos
    here = lax.axis_index(axis)
    return {axis: here + mask * (1 - 2 * ((here // mask) % 2))}


def kernel(
    stages, offsets, low_bits,
    rhs, order, source, transfer, target, out,
    order_v, chosen, rhs_v, source_v, target_v, transfer_v, in_v, placed_v,
    sent, received, load_sem, rhs_sem, transfer_sem, send_sem, recv_sem,
):
    leaf_count, leaf_rows = order.shape
    chunks = rhs_v.shape[0]
    units = leaf_count * chunks
    levels = transfer.shape[0]
    rank = source_v.shape[1]
    count = len(stages)

    load_order = pltpu.make_async_copy(order, order_v, load_sem.at[0])
    load_source = pltpu.make_async_copy(source, source_v, load_sem.at[1])
    load_target = pltpu.make_async_copy(target, target_v, load_sem.at[2])

    def load_rhs(chunk):
        return pltpu.make_async_copy(
            rhs.at[:, pl.ds(pl.multiple_of(chunk * WIDTH, WIDTH), WIDTH)], rhs_v.at[chunk], rhs_sem.at[chunk]
        )

    def load_transfer(level):
        return pltpu.make_async_copy(
            transfer.at[level], transfer_v.at[level], transfer_sem.at[max(level - low_bits + 1, 0)]
        )

    low_slots = transfer_v.at[pl.ds(0, low_bits)]
    low_transfer = pltpu.make_async_copy(low_slots, low_slots, transfer_sem.at[0])

    def select(leaf):
        grid_row = lax.broadcasted_iota(jnp.int32, (leaf_rows, leaf_rows), 0)
        named = jnp.broadcast_to(order_v[pl.ds(leaf, 1), :], (leaf_rows, leaf_rows))
        chosen[leaf] = jnp.where(grid_row == named, 1.0, 0.0).astype(BF16)

    def place_in(leaf):
        parts = jnp.concatenate(split(source_v[leaf]), axis=0)
        in_v[leaf] = lax.dot_general(
            parts, chosen[leaf], (((1,), (1,)), ((), ())), preferred_element_type=F32
        ).astype(BF16)

    def place_out(leaf):
        for index, part in enumerate(split(target_v[leaf])):
            placed_v[leaf, index] = lax.dot_general(
                chosen[leaf], part, (((1,), (1,)), ((), ())), preferred_element_type=F32
            ).astype(BF16)

    def exchange(stage, unit):
        return pltpu.make_async_remote_copy(
            src_ref=sent.at[stage, unit],
            dst_ref=received.at[stage, unit],
            send_sem=send_sem,
            recv_sem=recv_sem.at[stage, unit % FLIGHT],
            device_id=partner_id(*stages[stage]),
            device_id_type=pl.DeviceIdType.MESH,
        )

    def combine(level, node, own, other):
        return dot3(*split(transfer_v[level, node]), jnp.concatenate([own, other], axis=0))

    def enter(chunk, first=False):
        load_rhs(chunk).wait()
        current = {}
        for leaf in range(leaf_count):
            rows = rhs_v[chunk, pl.ds(leaf * leaf_rows, leaf_rows), :]
            current[0, leaf] = dot3(in_v[leaf, :rank], in_v[leaf, rank:], rows)

        def value_of(level, node):
            if (level, node) not in current:
                bit = level - 1
                current[level, node] = combine(bit, node, value_of(bit, node), value_of(bit, node ^ 2**bit))
            return current[level, node]

        for node in range(leaf_count):
            unit = chunk * leaf_count + node
            sent[0, unit] = value_of(low_bits, node)
            if first and node == 0:
                pl.semaphore_wait(barrier, count)
            if first and node < LEAD:
                exchange(0, unit).start()

    def advance(stage, unit):
        node = unit % leaf_count
        exchange(stage, unit).wait_recv()
        if stage == 0:

            @pl.when(unit + LEAD < units)
            def _():
                exchange(0, unit + LEAD).start()

        value = combine(low_bits + stage, node, sent[stage, unit], received[stage, unit])
        if stage + 1 < count:
            sent[stage + 1, unit] = value
            exchange(stage + 1, unit).start()
        else:
            chunk = unit // leaf_count
            rows = pl.ds(pl.multiple_of(node * leaf_rows, leaf_rows), leaf_rows)
            cols = pl.ds(pl.multiple_of(chunk * WIDTH, WIDTH), WIDTH)
            out[rows, cols] = dot3(placed_v[node, 0], placed_v[node, 1], value)

    load_order.start()
    load_source.start()
    barrier = pltpu.get_barrier_semaphore()
    for stage in stages:
        pl.semaphore_signal(barrier, inc=1, device_id=partner_id(*stage), device_id_type=pl.DeviceIdType.MESH)
    load_order.wait()
    load_rhs(0).start()
    for level in range(low_bits):
        load_transfer(level).start()
    for leaf in range(leaf_count):
        select(leaf)
    load_transfer(low_bits).start()
    load_rhs(1).start()
    load_source.wait()
    for leaf in range(leaf_count):
        place_in(leaf)
    if low_bits:
        low_transfer.wait()
    enter(0, first=True)
    for level in range(low_bits + 1, levels):
        load_transfer(level).start()
    load_target.start()
    for chunk in range(2, chunks):
        load_rhs(chunk).start()
    enter(1)

    near = [stage for stage in range(count) if stages[stage] == ("col", 0)]
    turns = near + [stage for stage in reversed(range(count)) if stage not in near]

    @pl.loop(0, units + offsets[-1])
    def _(tick):
        for stage in turns:
            unit = tick - offsets[stage]

            @pl.when(unit == 0)
            def _():
                load_transfer(low_bits + stage).wait()

            @pl.when((unit >= 0) & (unit < units))
            def _():
                advance(stage, unit)

        @pl.when((tick >= offsets[-1] - leaf_count) & (tick < offsets[-1]))
        def _():
            leaf = tick - (offsets[-1] - leaf_count)

            @pl.when(leaf == 0)
            def _():
                load_target.wait()

            place_out(leaf)

        @pl.when((tick % leaf_count == 1) & (tick > leaf_count) & (tick // leaf_count + 1 < chunks))
        def _():
            enter(tick // leaf_count + 1)

    pltpu.make_async_copy(sent, sent, send_sem).wait()


def output_kernel(result, out, sem):
    pieces = sem.shape[0]
    rows = out.shape[0] // pieces

    def store(piece):
        at = pl.ds(piece * rows, rows)
        return pltpu.make_async_copy(result.at[at, :], out.at[at, :], sem.at[piece])

    for piece in range(pieces):
        store(piece).start()
    for piece in range(pieces):
        store(piece).wait()


def on_device(rhs_grid, leaf_order, source_basis, transfer, target_basis):
    leaf_count, leaf_rows = leaf_order.shape
    points, columns = rhs_grid.shape
    rank = source_basis.shape[2]
    levels = transfer.shape[0]
    low_bits = leaf_count.bit_length() - 1
    row_bits = lax.axis_size("row").bit_length() - 1
    col_bits = lax.axis_size("col").bit_length() - 1
    stages = [("row", bit) for bit in range(row_bits)] + [("col", bit) for bit in range(col_bits)]
    count = len(stages)
    offsets = [0]
    for axis, bit in stages[1:]:
        if axis == "col":
            offsets.append(offsets[-1] + (NEAR if bit == 0 else LAST))
        else:
            offsets.append(offsets[-1] + (FAR if bit == row_bits - 1 else MIDDLE))
    chunks = columns // WIDTH
    units = leaf_count * chunks
    hbm = pl.BlockSpec(memory_space=pl.ANY)
    vmem = pl.BlockSpec(memory_space=pltpu.VMEM)
    result = pl.pallas_call(
        functools.partial(kernel, stages, offsets, low_bits),
        out_shape=pltpu.VMEM((points, columns), F32),
        in_specs=[hbm, hbm, hbm, hbm, hbm],
        out_specs=vmem,
        scratch_shapes=[
            pltpu.VMEM((leaf_count, leaf_rows), jnp.int32),
            pltpu.VMEM((leaf_count, leaf_rows, leaf_rows), BF16),
            pltpu.VMEM((chunks, points, WIDTH), F32),
            pltpu.VMEM((leaf_count, rank, leaf_rows), F32),
            pltpu.VMEM((leaf_count, rank, leaf_rows), F32),
            pltpu.VMEM(transfer.shape, F32),
            pltpu.VMEM((leaf_count, 2 * rank, leaf_rows), BF16),
            pltpu.VMEM((leaf_count, 2, leaf_rows, rank), BF16),
            pltpu.VMEM((count, units, rank, WIDTH), F32),
            pltpu.VMEM((count, units, rank, WIDTH), F32),
            pltpu.SemaphoreType.DMA((3,)),
            pltpu.SemaphoreType.DMA((chunks,)),
            pltpu.SemaphoreType.DMA((count + 1,)),
            pltpu.SemaphoreType.DMA,
            pltpu.SemaphoreType.DMA((count, FLIGHT)),
        ],
        compiler_params=pltpu.CompilerParams(
            collective_id=0, has_side_effects=True, vmem_limit_bytes=VMEM_BYTES - 4 * points * columns - 2**18
        ),
    )(rhs_grid, leaf_order, source_basis.swapaxes(1, 2), transfer, target_basis.swapaxes(1, 2))
    return pl.pallas_call(
        output_kernel,
        out_shape=jax.ShapeDtypeStruct((points, columns), F32),
        in_specs=[vmem],
        out_specs=hbm,
        scratch_shapes=[pltpu.SemaphoreType.DMA((2 * leaf_count,))],
        compiler_params=pltpu.CompilerParams(vmem_limit_bytes=2**20),
    )(result)


def solution(mesh):
    in_specs = (
        P(("row", "col"), None),
        P(("row", "col"), None),
        P(("row", "col"), None, None),
        P(None, ("row", "col"), None, None),
        P(("row", "col"), None, None),
    )
    out_specs = P(("row", "col"), None)
    return jax.shard_map(
        on_device, mesh=mesh, in_specs=in_specs, out_specs=out_specs, check_vma=False
    )
```

```python
import functools

import jax
import jax.numpy as jnp
from jax import lax
from jax.experimental import pallas as pl
from jax.experimental.pallas import tpu as pltpu
from jax.sharding import PartitionSpec as P

F32 = jnp.float32
BF16 = jnp.bfloat16
WIDTH = 128
MIDDLE = 2
FAR = 3
NEAR = 1
LAST = 2
LEAD = 1
FLIGHT = 8
VMEM_BYTES = 67043328


def split(value):
    high = value.astype(BF16)
    return high, (value - high.astype(F32)).astype(BF16)


def dot(a, b):
    return jnp.dot(a, b, preferred_element_type=F32)


def dot3(a_high, a_low, b):
    b_high, b_low = split(b)
    width = b.shape[1]
    both = dot(a_high, jnp.concatenate([b_high, b_low], axis=1))
    return both[:, :width] + (both[:, width:] + dot(a_low, b_high))


def partner_id(axis, bit_pos):
    mask = 2**bit_pos
    here = lax.axis_index(axis)
    return {axis: here + mask * (1 - 2 * ((here // mask) % 2))}


def kernel(
    stages, offsets, low_bits,
    rhs, order, source, transfer, target, out,
    order_v, chosen, rhs_v, source_v, target_v, transfer_v, in_v, placed_v,
    sent, received, load_sem, rhs_sem, transfer_sem, send_sem, recv_sem,
):
    leaf_count, leaf_rows = order.shape
    chunks = rhs_v.shape[0]
    units = leaf_count * chunks
    levels = transfer.shape[0]
    rank = source_v.shape[1]
    count = len(stages)

    load_order = pltpu.make_async_copy(order, order_v, load_sem.at[0])
    load_source = pltpu.make_async_copy(source, source_v, load_sem.at[1])
    load_target = pltpu.make_async_copy(target, target_v, load_sem.at[2])

    def load_rhs(chunk):
        return pltpu.make_async_copy(
            rhs.at[:, pl.ds(pl.multiple_of(chunk * WIDTH, WIDTH), WIDTH)], rhs_v.at[chunk], rhs_sem.at[chunk]
        )

    def load_transfer(level):
        return pltpu.make_async_copy(
            transfer.at[level], transfer_v.at[level], transfer_sem.at[max(level - low_bits + 1, 0)]
        )

    low_slots = transfer_v.at[pl.ds(0, low_bits)]
    low_transfer = pltpu.make_async_copy(low_slots, low_slots, transfer_sem.at[0])

    def select(leaf):
        grid_row = lax.broadcasted_iota(jnp.int32, (leaf_rows, leaf_rows), 0)
        named = jnp.broadcast_to(order_v[pl.ds(leaf, 1), :], (leaf_rows, leaf_rows))
        chosen[leaf] = jnp.where(grid_row == named, 1.0, 0.0).astype(BF16)

    def place_in(leaf):
        parts = jnp.concatenate(split(source_v[leaf]), axis=0)
        in_v[leaf] = lax.dot_general(
            parts, chosen[leaf], (((1,), (1,)), ((), ())), preferred_element_type=F32
        ).astype(BF16)

    def place_out(leaf):
        for index, part in enumerate(split(target_v[leaf])):
            placed_v[leaf, index] = lax.dot_general(
                chosen[leaf], part, (((1,), (1,)), ((), ())), preferred_element_type=F32
            ).astype(BF16)

    def exchange(stage, unit):
        return pltpu.make_async_remote_copy(
            src_ref=sent.at[stage, unit],
            dst_ref=received.at[stage, unit],
            send_sem=send_sem,
            recv_sem=recv_sem.at[stage, unit % FLIGHT],
            device_id=partner_id(*stages[stage]),
            device_id_type=pl.DeviceIdType.MESH,
        )

    def combine(level, node, own, other):
        return dot3(*split(transfer_v[level, node]), jnp.concatenate([own, other], axis=0))

    def enter(chunk, first=False):
        load_rhs(chunk).wait()
        current = {}
        for leaf in range(leaf_count):
            rows = rhs_v[chunk, pl.ds(leaf * leaf_rows, leaf_rows), :]
            current[0, leaf] = dot3(in_v[leaf, :rank], in_v[leaf, rank:], rows)

        def value_of(level, node):
            if (level, node) not in current:
                bit = level - 1
                current[level, node] = combine(bit, node, value_of(bit, node), value_of(bit, node ^ 2**bit))
            return current[level, node]

        for node in range(leaf_count):
            unit = chunk * leaf_count + node
            sent[0, unit] = value_of(low_bits, node)
            if first and node == 0:
                pl.semaphore_wait(barrier, count)
            if first and node < LEAD:
                exchange(0, unit).start()

    def advance(stage, unit):
        node = unit % leaf_count
        exchange(stage, unit).wait_recv()
        if stage == 0:

            @pl.when(unit + LEAD < units)
            def _():
                exchange(0, unit + LEAD).start()

        value = combine(low_bits + stage, node, sent[stage, unit], received[stage, unit])
        if stage + 1 < count:
            sent[stage + 1, unit] = value
            exchange(stage + 1, unit).start()
        else:
            chunk = unit // leaf_count
            rows = pl.ds(pl.multiple_of(node * leaf_rows, leaf_rows), leaf_rows)
            cols = pl.ds(pl.multiple_of(chunk * WIDTH, WIDTH), WIDTH)
            out[rows, cols] = dot3(placed_v[node, 0], placed_v[node, 1], value)

    load_order.start()
    load_source.start()
    barrier = pltpu.get_barrier_semaphore()
    for stage in stages:
        pl.semaphore_signal(barrier, inc=1, device_id=partner_id(*stage), device_id_type=pl.DeviceIdType.MESH)
    load_order.wait()
    load_rhs(0).start()
    for level in range(low_bits):
        load_transfer(level).start()
    for leaf in range(leaf_count):
        select(leaf)
    load_transfer(low_bits).start()
    load_rhs(1).start()
    load_source.wait()
    for leaf in range(leaf_count):
        place_in(leaf)
    if low_bits:
        low_transfer.wait()
    enter(0, first=True)
    for level in range(low_bits + 1, levels):
        load_transfer(level).start()
    load_target.start()
    for chunk in range(2, chunks):
        load_rhs(chunk).start()
    enter(1)

    near = [stage for stage in range(count) if stages[stage] == ("col", 0)]
    turns = near + [stage for stage in reversed(range(count)) if stage not in near]

    behind = lax.axis_index("col") % 2

    @pl.loop(0, units + offsets[-1] + 1)
    def _(tick):
        for stage in turns:
            unit = tick - offsets[stage] - (behind if near and stage >= near[0] else 0)

            @pl.when(unit == 0)
            def _():
                load_transfer(low_bits + stage).wait()

            @pl.when((unit >= 0) & (unit < units))
            def _():
                advance(stage, unit)

        @pl.when((tick >= offsets[-1] - leaf_count) & (tick < offsets[-1]))
        def _():
            leaf = tick - (offsets[-1] - leaf_count)

            @pl.when(leaf == 0)
            def _():
                load_target.wait()

            place_out(leaf)

        @pl.when((tick % leaf_count == 1) & (tick > leaf_count) & (tick // leaf_count + 1 < chunks))
        def _():
            enter(tick // leaf_count + 1)

    pltpu.make_async_copy(sent, sent, send_sem).wait()


def output_kernel(result, out, sem):
    pieces = sem.shape[0]
    rows = out.shape[0] // pieces

    def store(piece):
        at = pl.ds(piece * rows, rows)
        return pltpu.make_async_copy(result.at[at, :], out.at[at, :], sem.at[piece])

    for piece in range(pieces):
        store(piece).start()
    for piece in range(pieces):
        store(piece).wait()


def on_device(rhs_grid, leaf_order, source_basis, transfer, target_basis):
    leaf_count, leaf_rows = leaf_order.shape
    points, columns = rhs_grid.shape
    rank = source_basis.shape[2]
    levels = transfer.shape[0]
    low_bits = leaf_count.bit_length() - 1
    row_bits = lax.axis_size("row").bit_length() - 1
    col_bits = lax.axis_size("col").bit_length() - 1
    stages = [("row", bit) for bit in range(row_bits)] + [("col", bit) for bit in range(col_bits)]
    count = len(stages)
    offsets = [0]
    for axis, bit in stages[1:]:
        if axis == "col":
            offsets.append(offsets[-1] + (NEAR if bit == 0 else LAST))
        else:
            offsets.append(offsets[-1] + (FAR if bit == row_bits - 1 else MIDDLE))
    chunks = columns // WIDTH
    units = leaf_count * chunks
    hbm = pl.BlockSpec(memory_space=pl.ANY)
    vmem = pl.BlockSpec(memory_space=pltpu.VMEM)
    result = pl.pallas_call(
        functools.partial(kernel, stages, offsets, low_bits),
        out_shape=pltpu.VMEM((points, columns), F32),
        in_specs=[hbm, hbm, hbm, hbm, hbm],
        out_specs=vmem,
        scratch_shapes=[
            pltpu.VMEM((leaf_count, leaf_rows), jnp.int32),
            pltpu.VMEM((leaf_count, leaf_rows, leaf_rows), BF16),
            pltpu.VMEM((chunks, points, WIDTH), F32),
            pltpu.VMEM((leaf_count, rank, leaf_rows), F32),
            pltpu.VMEM((leaf_count, rank, leaf_rows), F32),
            pltpu.VMEM(transfer.shape, F32),
            pltpu.VMEM((leaf_count, 2 * rank, leaf_rows), BF16),
            pltpu.VMEM((leaf_count, 2, leaf_rows, rank), BF16),
            pltpu.VMEM((count, units, rank, WIDTH), F32),
            pltpu.VMEM((count, units, rank, WIDTH), F32),
            pltpu.SemaphoreType.DMA((3,)),
            pltpu.SemaphoreType.DMA((chunks,)),
            pltpu.SemaphoreType.DMA((count + 1,)),
            pltpu.SemaphoreType.DMA,
            pltpu.SemaphoreType.DMA((count, FLIGHT)),
        ],
        compiler_params=pltpu.CompilerParams(
            collective_id=0, has_side_effects=True, vmem_limit_bytes=VMEM_BYTES - 4 * points * columns - 2**18
        ),
    )(rhs_grid, leaf_order, source_basis.swapaxes(1, 2), transfer, target_basis.swapaxes(1, 2))
    return pl.pallas_call(
        output_kernel,
        out_shape=jax.ShapeDtypeStruct((points, columns), F32),
        in_specs=[vmem],
        out_specs=hbm,
        scratch_shapes=[pltpu.SemaphoreType.DMA((2 * leaf_count,))],
        compiler_params=pltpu.CompilerParams(vmem_limit_bytes=2**20),
    )(result)


def solution(mesh):
    in_specs = (
        P(("row", "col"), None),
        P(("row", "col"), None),
        P(("row", "col"), None, None),
        P(None, ("row", "col"), None, None),
        P(("row", "col"), None, None),
    )
    out_specs = P(("row", "col"), None)
    return jax.shard_map(
        on_device, mesh=mesh, in_specs=in_specs, out_specs=out_specs, check_vma=False
    )
```

```python
import functools

import jax
import jax.numpy as jnp
from jax import lax
from jax.experimental import pallas as pl
from jax.experimental.pallas import tpu as pltpu
from jax.sharding import PartitionSpec as P

F32 = jnp.float32
BF16 = jnp.bfloat16
WIDTH = 128
MIDDLE = 2
FAR = 3
NEAR = 1
LAST = 2
LEAD = 1
FLIGHT = 6
VMEM_BYTES = 67043328


def split(value):
    high = value.astype(BF16)
    return high, (value - high.astype(F32)).astype(BF16)


def dot(a, b):
    return jnp.dot(a, b, preferred_element_type=F32)


def dot3(a_high, a_low, b):
    b_high, b_low = split(b)
    width = b.shape[1]
    both = dot(a_high, jnp.concatenate([b_high, b_low], axis=1))
    return both[:, :width] + (both[:, width:] + dot(a_low, b_high))


def partner_id(axis, bit_pos):
    mask = 2**bit_pos
    here = lax.axis_index(axis)
    return {axis: here + mask * (1 - 2 * ((here // mask) % 2))}


def kernel(
    stages, offsets, low_bits,
    rhs, order, source, transfer, target, out,
    order_v, chosen, rhs_v, source_v, target_v, transfer_v, in_v, placed_v,
    sent, received, load_sem, rhs_sem, transfer_sem, send_sem, recv_sem,
):
    leaf_count, leaf_rows = order.shape
    chunks = rhs_v.shape[0]
    units = leaf_count * chunks
    levels = transfer.shape[0]
    rank = source_v.shape[1]
    count = len(stages)

    load_order = pltpu.make_async_copy(order, order_v, load_sem.at[0])
    load_source = pltpu.make_async_copy(source, source_v, load_sem.at[1])
    load_target = pltpu.make_async_copy(target, target_v, load_sem.at[2])

    def load_rhs(chunk):
        return pltpu.make_async_copy(
            rhs.at[:, pl.ds(pl.multiple_of(chunk * WIDTH, WIDTH), WIDTH)], rhs_v.at[chunk], rhs_sem.at[chunk]
        )

    def load_transfer(level):
        return pltpu.make_async_copy(
            transfer.at[level], transfer_v.at[level], transfer_sem.at[max(level - low_bits + 1, 0)]
        )

    low_slots = transfer_v.at[pl.ds(0, low_bits)]
    low_transfer = pltpu.make_async_copy(low_slots, low_slots, transfer_sem.at[0])

    def select(leaf):
        grid_row = lax.broadcasted_iota(jnp.int32, (leaf_rows, leaf_rows), 0)
        named = jnp.broadcast_to(order_v[pl.ds(leaf, 1), :], (leaf_rows, leaf_rows))
        chosen[leaf] = jnp.where(grid_row == named, 1.0, 0.0).astype(BF16)

    def place_in(leaf):
        parts = jnp.concatenate(split(source_v[leaf]), axis=0)
        in_v[leaf] = lax.dot_general(
            parts, chosen[leaf], (((1,), (1,)), ((), ())), preferred_element_type=F32
        ).astype(BF16)

    def place_out(leaf):
        for index, part in enumerate(split(target_v[leaf])):
            placed_v[leaf, index] = lax.dot_general(
                chosen[leaf], part, (((1,), (1,)), ((), ())), preferred_element_type=F32
            ).astype(BF16)

    def exchange(stage, unit):
        return pltpu.make_async_remote_copy(
            src_ref=sent.at[stage, unit],
            dst_ref=received.at[stage, unit],
            send_sem=send_sem,
            recv_sem=recv_sem.at[stage, unit % FLIGHT],
            device_id=partner_id(*stages[stage]),
            device_id_type=pl.DeviceIdType.MESH,
        )

    def combine(level, node, own, other):
        return dot3(*split(transfer_v[level, node]), jnp.concatenate([own, other], axis=0))

    def enter(chunk, first=False):
        load_rhs(chunk).wait()
        current = {}
        for leaf in range(leaf_count):
            rows = rhs_v[chunk, pl.ds(leaf * leaf_rows, leaf_rows), :]
            current[0, leaf] = dot3(in_v[leaf, :rank], in_v[leaf, rank:], rows)

        def value_of(level, node):
            if (level, node) not in current:
                bit = level - 1
                current[level, node] = combine(bit, node, value_of(bit, node), value_of(bit, node ^ 2**bit))
            return current[level, node]

        for node in range(leaf_count):
            unit = chunk * leaf_count + node
            sent[0, unit] = value_of(low_bits, node)
            if first and node == 0:
                pl.semaphore_wait(barrier, count)
            if first and node < LEAD:
                exchange(0, unit).start()

    def advance(stage, unit):
        node = unit % leaf_count
        exchange(stage, unit).wait_recv()
        if stage == 0:

            @pl.when(unit + LEAD < units)
            def _():
                exchange(0, unit + LEAD).start()

        value = combine(low_bits + stage, node, sent[stage, unit], received[stage, unit])
        if stage + 1 < count:
            sent[stage + 1, unit] = value
            exchange(stage + 1, unit).start()
        else:
            chunk = unit // leaf_count
            rows = pl.ds(pl.multiple_of(node * leaf_rows, leaf_rows), leaf_rows)
            cols = pl.ds(pl.multiple_of(chunk * WIDTH, WIDTH), WIDTH)
            out[rows, cols] = dot3(placed_v[node, 0], placed_v[node, 1], value)

    load_order.start()
    load_source.start()
    barrier = pltpu.get_barrier_semaphore()
    for stage in stages:
        pl.semaphore_signal(barrier, inc=1, device_id=partner_id(*stage), device_id_type=pl.DeviceIdType.MESH)
    load_order.wait()
    load_rhs(0).start()
    for level in range(low_bits):
        load_transfer(level).start()
    for leaf in range(leaf_count):
        select(leaf)
    load_transfer(low_bits).start()
    load_rhs(1).start()
    load_source.wait()
    for leaf in range(leaf_count):
        place_in(leaf)
    if low_bits:
        low_transfer.wait()
    enter(0, first=True)
    for level in range(low_bits + 1, levels):
        load_transfer(level).start()
    load_target.start()
    for chunk in range(2, chunks):
        load_rhs(chunk).start()
    enter(1)

    near = [stage for stage in range(count) if stages[stage] == ("col", 0)]
    turns = near + [stage for stage in reversed(range(count)) if stage not in near]

    behind = lax.axis_index("col") % 2

    @pl.loop(0, units + offsets[-1] + 1)
    def _(tick):
        for stage in turns:
            unit = tick - offsets[stage] - (behind if near and stage >= near[0] else 0)

            @pl.when(unit == 0)
            def _():
                load_transfer(low_bits + stage).wait()

            @pl.when((unit >= 0) & (unit < units))
            def _():
                advance(stage, unit)

        @pl.when((tick >= offsets[-1] - leaf_count) & (tick < offsets[-1]))
        def _():
            leaf = tick - (offsets[-1] - leaf_count)

            @pl.when(leaf == 0)
            def _():
                load_target.wait()

            place_out(leaf)

        @pl.when((tick % leaf_count == 1) & (tick > leaf_count) & (tick // leaf_count + 1 < chunks))
        def _():
            enter(tick // leaf_count + 1)

    pltpu.make_async_copy(sent, sent, send_sem).wait()


def output_kernel(result, out, sem):
    pieces = sem.shape[0]
    rows = out.shape[0] // pieces

    def store(piece):
        at = pl.ds(piece * rows, rows)
        return pltpu.make_async_copy(result.at[at, :], out.at[at, :], sem.at[piece])

    for piece in range(pieces):
        store(piece).start()
    for piece in range(pieces):
        store(piece).wait()


def on_device(rhs_grid, leaf_order, source_basis, transfer, target_basis):
    leaf_count, leaf_rows = leaf_order.shape
    points, columns = rhs_grid.shape
    rank = source_basis.shape[2]
    levels = transfer.shape[0]
    low_bits = leaf_count.bit_length() - 1
    row_bits = lax.axis_size("row").bit_length() - 1
    col_bits = lax.axis_size("col").bit_length() - 1
    stages = [("row", bit) for bit in range(row_bits)] + [("col", bit) for bit in range(col_bits)]
    count = len(stages)
    offsets = [0]
    for axis, bit in stages[1:]:
        if axis == "col":
            offsets.append(offsets[-1] + (NEAR if bit == 0 else LAST))
        else:
            offsets.append(offsets[-1] + (FAR if bit == row_bits - 1 else MIDDLE))
    chunks = columns // WIDTH
    units = leaf_count * chunks
    hbm = pl.BlockSpec(memory_space=pl.ANY)
    vmem = pl.BlockSpec(memory_space=pltpu.VMEM)
    result = pl.pallas_call(
        functools.partial(kernel, stages, offsets, low_bits),
        out_shape=pltpu.VMEM((points, columns), F32),
        in_specs=[hbm, hbm, hbm, hbm, hbm],
        out_specs=vmem,
        scratch_shapes=[
            pltpu.VMEM((leaf_count, leaf_rows), jnp.int32),
            pltpu.VMEM((leaf_count, leaf_rows, leaf_rows), BF16),
            pltpu.VMEM((chunks, points, WIDTH), F32),
            pltpu.VMEM((leaf_count, rank, leaf_rows), F32),
            pltpu.VMEM((leaf_count, rank, leaf_rows), F32),
            pltpu.VMEM(transfer.shape, F32),
            pltpu.VMEM((leaf_count, 2 * rank, leaf_rows), BF16),
            pltpu.VMEM((leaf_count, 2, leaf_rows, rank), BF16),
            pltpu.VMEM((count, units, rank, WIDTH), F32),
            pltpu.VMEM((count, units, rank, WIDTH), F32),
            pltpu.SemaphoreType.DMA((3,)),
            pltpu.SemaphoreType.DMA((chunks,)),
            pltpu.SemaphoreType.DMA((count + 1,)),
            pltpu.SemaphoreType.DMA,
            pltpu.SemaphoreType.DMA((count, FLIGHT)),
        ],
        compiler_params=pltpu.CompilerParams(
            collective_id=0, has_side_effects=True, vmem_limit_bytes=VMEM_BYTES - 4 * points * columns - 2**18
        ),
    )(rhs_grid, leaf_order, source_basis.swapaxes(1, 2), transfer, target_basis.swapaxes(1, 2))
    return pl.pallas_call(
        output_kernel,
        out_shape=jax.ShapeDtypeStruct((points, columns), F32),
        in_specs=[vmem],
        out_specs=hbm,
        scratch_shapes=[pltpu.SemaphoreType.DMA((2 * leaf_count,))],
        compiler_params=pltpu.CompilerParams(vmem_limit_bytes=2**20),
    )(result)


def solution(mesh):
    in_specs = (
        P(("row", "col"), None),
        P(("row", "col"), None),
        P(("row", "col"), None, None),
        P(None, ("row", "col"), None, None),
        P(("row", "col"), None, None),
    )
    out_specs = P(("row", "col"), None)
    return jax.shard_map(
        on_device, mesh=mesh, in_specs=in_specs, out_specs=out_specs, check_vma=False
    )
```
